32 devices in a mesh: wide: 16 (over z, y, x), narrow: 2 (over core).
Axes of the slice: x: 2, y: 2, z: 4, core: 2. Of those that a mesh axis runs over, the one named last changes fastest.
Arguments:
- tokens: bfloat16 [6144, 2048], P(('wide', 'narrow')), may hold values from -6 to 6
- noise_embed: float32 [3, 256], replicated, may hold values from -6 to 6
- qkv_weight: bfloat16 [2048, 6144], P('wide'), may hold values from -0.125 to 0.125
- out_weight: bfloat16 [2048, 2048], P('wide'), may hold values from -0.5 to 0.5
- out_bias: bfloat16 [2048], P('wide'), may hold values from -3 to 3
- up_weight: bfloat16 [2048, 8192], P('wide'), may hold values from -0.125 to 0.125
- up_bias: bfloat16 [8192], P('wide'), may hold values from -3 to 3
- down_weight: bfloat16 [8192, 2048], P('wide'), may hold values from -0.0625 to 0.0625
- down_bias: bfloat16 [2048], P('wide'), may hold values from -3 to 3
- mod_weight: bfloat16 [256, 12288], P('wide'), may hold values from -0.375 to 0.375
- mod_bias: bfloat16 [12288], P('wide'), may hold values from -3 to 3
- cotangent: bfloat16 [6144, 2048], P(('wide', 'narrow')), may hold values from -6 to 6
- image_device: int32 [88], replicated, may hold values from 0 to 31, as said below
- image_offset: int32 [88], replicated, may hold values from 0 to 160
- image_length: int32 [88], replicated, may hold values from 8 to 128, as said below
- image_group: int32 [88], replicated, may hold values from 0 to 2, as said below
Outputs:
- output: bfloat16 [6144, 2048], P(('wide', 'narrow'))
- tokens_grad: bfloat16 [6144, 2048], P(('wide', 'narrow'))
- noise_grad: float32 [3, 256], P(None, 'wide')
- qkv_grad: float32 [2048, 6144], P('wide')
- out_grad: float32 [2048, 2048], P('wide')
- out_bias_grad: float32 [2048], P('wide')
- up_grad: float32 [2048, 8192], P('wide')
- up_bias_grad: float32 [8192], P('wide')
- down_grad: float32 [8192, 2048], P('wide')
- down_bias_grad: float32 [2048], P('wide')
- mod_grad: float32 [256, 12288], P('wide')
- mod_bias_grad: float32 [12288], P('wide')
The draws below stay inside these ranges and needn't reach their ends.
Inputs may be any that keep to these rules, and one draw needn't show every extreme that they name: `image_device`: each image lies whole in one device's buffer. Every device holds one of four loads, a quarter of the devices each: an image of 128 tokens followed by two of 32; one image of 128; two images of 32; or one of 32 followed by four of 8. A buffer's images start at row 0 and follow one another without gaps; the rows after them are unused. `image_length`: every length is 128, 32 or 8. `image_group`: images of 128 tokens are of group 0, of 32 of group 1, of 8 of group 2.
All inputs are finite; a program needn't handle non-finite values.
Results may differ from the reference program's by a relative error of at most 0.02.
Values may be sent and summed in bfloat16 or wider, within the bound.
No kernel may reach another device: no remote copies, remote signals or barrier semaphores. Data moves between devices by JAX's collectives and lax.ppermute only.
A program may use at most 384 MiB of HBM per device.

```python
import jax
import jax.numpy as jnp
from jax import lax

D = 2048
HEADS = 16
HEAD_DIM = 128
FF = 8192
EMB = 256
GROUPS = 3
SHORT_LEN = 8
CAP = 192
SLOTS = 6144
IMAGES = 88
DEVICES = 32


def placement_tables(key):
    base = jax.random.fold_in(key, 7)
    first_key, second_key = jax.random.split(base)
    device_order = jax.random.permutation(first_key, DEVICES).astype(jnp.int32)
    kind_table = jnp.array([0, 0, 0, 1, 2, 2, 3, 3, 3, 3, 3], jnp.int32)
    unit_offsets = jnp.array([0, 16, 20, 0, 0, 4, 0, 4, 5, 6, 7], jnp.int32)
    unit_lengths = jnp.array([16, 4, 4, 16, 4, 4, 4, 1, 1, 1, 1], jnp.int32)
    group_table = jnp.array([0, 1, 1, 0, 1, 1, 1, 2, 2, 2, 2], jnp.int32)
    quad_count = DEVICES // 4
    quad_ids = jnp.arange(quad_count, dtype=jnp.int32)[:, None]
    devices_all = device_order[4 * quad_ids + kind_table[None, :]].reshape(-1)
    offsets_all = jnp.broadcast_to(unit_offsets[None, :] * SHORT_LEN, (quad_count, 11)).reshape(-1)
    lengths_all = jnp.broadcast_to(unit_lengths[None, :] * SHORT_LEN, (quad_count, 11)).reshape(-1)
    groups_all = jnp.broadcast_to(group_table[None, :], (quad_count, 11)).reshape(-1)
    shuffle = jax.random.permutation(second_key, IMAGES).astype(jnp.int32)
    return (devices_all[shuffle], offsets_all[shuffle], lengths_all[shuffle], groups_all[shuffle])


def draw_image_device(key, part):
    return placement_tables(key)[0]


def draw_image_offset(key, part):
    return placement_tables(key)[1]


def draw_image_length(key, part):
    return placement_tables(key)[2]


def draw_image_group(key, part):
    return placement_tables(key)[3]


def block_levels(rng, dims, cuts, low, top_value):
    factor_of, own = 1.0, jax.random.fold_in(rng, 6)
    for position, shards_of in cuts:
        steps = jnp.exp(jax.random.uniform(jax.random.fold_in(own, position), (shards_of,), jnp.float32, low / len(cuts), top_value / len(cuts)))
        factor_of = factor_of * jnp.repeat(steps, dims[position] // shards_of).reshape([-1 if axis == position else 1 for axis in range(len(dims))])
    return factor_of


def scatter_about(stream_key, extent, deviation, most, cuts=(), kind=jnp.bfloat16):
    values = jax.random.normal(stream_key, extent, jnp.float32) * deviation
    if len(cuts) > 0:
        values = block_levels(stream_key, extent, cuts, -0.22, 0.18) * values
    return jnp.clip(values, min=-most, max=most).astype(kind)


def setup_inputs(seed: int = 0) -> dict:
    streams_of = jax.random.split(jax.random.key(seed), 17)
    return {
        "tokens": scatter_about(streams_of[0], (SLOTS, D), 1.0, 6.0, ((0, 32),)),
        "noise_embed": scatter_about(streams_of[1], (GROUPS, EMB), 1.0, 6.0, (), jnp.float32),
        "qkv_weight": scatter_about(streams_of[2], (D, 3 * D), D ** -0.5, 0.125, ((0, 16),)),
        "out_weight": scatter_about(streams_of[3], (D, D), (D // 16) ** -0.5, 0.5, ((0, 16),)),
        "out_bias": scatter_about(streams_of[4], (D,), 0.5, 3.0, ((0, 16),)),
        "up_weight": scatter_about(streams_of[5], (D, FF), D ** -0.5, 0.125, ((0, 16),)),
        "up_bias": scatter_about(streams_of[6], (FF,), 0.5, 3.0, ((0, 16),)),
        "down_weight": scatter_about(streams_of[7], (FF, D), FF ** -0.5, 0.0625, ((0, 16),)),
        "down_bias": scatter_about(streams_of[8], (D,), 0.5, 3.0, ((0, 16),)),
        "mod_weight": scatter_about(streams_of[9], (EMB, 6 * D), EMB ** -0.5, 0.375, ((0, 16),)),
        "mod_bias": scatter_about(streams_of[10], (6 * D,), 0.5, 3.0, ((0, 16),)),
        "cotangent": scatter_about(streams_of[11], (SLOTS, D), 1.0, 6.0, ((0, 32),)),
        "image_device": draw_image_device(jax.random.fold_in(streams_of[16], 71), 0),
        "image_offset": draw_image_offset(jax.random.fold_in(streams_of[16], 71), 0),
        "image_length": draw_image_length(jax.random.fold_in(streams_of[16], 71), 0),
        "image_group": draw_image_group(jax.random.fold_in(streams_of[16], 71), 0),
    }


highest = lax.Precision.HIGHEST

@jax.custom_vjp
def low(v):
    return lax.optimization_barrier(v.astype(jnp.bfloat16)).astype(jnp.float32)

@jax.custom_vjp
def low_back(v):
    return v

def low_keep(v):
    return (low(v), None)

def low_pass(kept, grad):
    return (grad,)

def back_keep(v):
    return (v, None)

def back_low(kept, grad):
    return (low(grad),)
low.defvjp(low_keep, low_pass)
low_back.defvjp(back_keep, back_low)

def matmul(left, right):
    return jnp.dot(left, right, precision=highest, preferred_element_type=jnp.float32)

def layer_norm(values):
    centred = values - lax.optimization_barrier(jnp.mean(values, axis=-1, keepdims=True))
    return centred * lax.rsqrt(lax.optimization_barrier(jnp.mean(centred * centred, axis=-1, keepdims=True)) + 1e-06)

def slot_tables(device, image_device, image_offset, image_length, image_group):
    slot_ids = jnp.arange(CAP, dtype=jnp.int32)[:, None]
    starts = image_offset[None, :]
    inside = (image_device[None, :] == device) & (slot_ids >= starts) & (slot_ids < starts + image_length[None, :])
    numbers = jnp.arange(image_device.shape[0], dtype=jnp.int32)[None, :]
    segment = lax.optimization_barrier(jnp.sum(jnp.where(inside, numbers + 1, 0), axis=1)) - 1
    usable = jnp.any(inside, axis=1)
    group_slot = lax.optimization_barrier(jnp.sum(jnp.where(inside, image_group[None, :], 0), axis=1))
    onehot = (group_slot[:, None] == jnp.arange(GROUPS, dtype=jnp.int32)[None, :]) & usable[:, None]
    return (segment, usable.astype(jnp.float32), onehot.astype(jnp.float32))

def attention(queries, key_rows, value_rows, same):
    raw_scores = jnp.einsum('qhd,khd->hqk', queries, key_rows, precision=highest) * HEAD_DIM ** (-0.5)
    scores = low_back(raw_scores)
    masked = jnp.where(same[None], scores, -1e+30)
    row_max = lax.optimization_barrier(jnp.max(masked, axis=-1, keepdims=True))
    powers = jnp.exp(masked - row_max)
    attend = powers / lax.optimization_barrier(jnp.sum(powers, axis=-1, keepdims=True))
    return jnp.einsum('hqk,khd->qhd', low(attend), value_rows, precision=highest)

def reference(tokens, noise_embed, qkv_weight, out_weight, out_bias, up_weight, up_bias, down_weight, down_bias, mod_weight, mod_bias, cotangent, image_device, image_offset, image_length, image_group):

    def layer_block(x_rows, device, modulation, weights):
        qkv_f, out_f, out_bias_f, up_f, up_bias_f, down_f, down_bias_f = weights
        segment, usable, onehot = slot_tables(device, image_device, image_offset, image_length, image_group)
        token_mod = matmul(onehot, modulation)
        shift_a, scale_a, gate_a, shift_b, scale_b, gate_b = jnp.split(token_mod, 6, axis=1)
        modulated_a = low(layer_norm(x_rows) * (1.0 + scale_a) + shift_a)
        projected = low_back(low(matmul(modulated_a, qkv_f)))
        query_part, key_part, value_part = jnp.split(projected, 3, axis=1)
        queries = query_part.reshape(CAP, HEADS, HEAD_DIM)
        key_rows = key_part.reshape(CAP, HEADS, HEAD_DIM)
        value_rows = value_part.reshape(CAP, HEADS, HEAD_DIM)
        same = segment[:, None] == segment[None, :]
        context = low_back(low(attention(queries, key_rows, value_rows, same).reshape(CAP, D)))
        branch_a = low_back(matmul(context, out_f) + out_bias_f)
        residual = x_rows + gate_a * branch_a
        modulated_b = low(layer_norm(residual) * (1.0 + scale_b) + shift_b)
        hidden_pre = low_back(matmul(modulated_b, up_f) + up_bias_f)
        hidden = low(jax.nn.gelu(hidden_pre))
        branch_b = low_back(matmul(hidden, down_f) + down_bias_f)
        return (residual + gate_b * branch_b) * usable[:, None]

    def forward(tokens_f, noise_f, qkv_f, out_f, out_bias_f, up_f, up_bias_f, down_f, down_bias_f, mod_f, mod_bias_f):
        modulation = low_back(matmul(low(jax.nn.silu(noise_f)), mod_f) + mod_bias_f)
        weights = (qkv_f, out_f, out_bias_f, up_f, up_bias_f, down_f, down_bias_f)
        run_block = jax.checkpoint(layer_block)

        def scan_step(carried, inputs):
            x_block, device = inputs
            return (carried, run_block(x_block, device, modulation, weights))
        blocks = tokens_f.reshape(DEVICES, CAP, D)
        carried_end, outputs = lax.scan(scan_step, jnp.zeros((), jnp.float32), (blocks, jnp.arange(DEVICES, dtype=jnp.int32)))
        return outputs.reshape(DEVICES * CAP, D)
    floats = (tokens, noise_embed, qkv_weight, out_weight, out_bias, up_weight, up_bias, down_weight, down_bias, mod_weight, mod_bias)
    floats = tuple((entry.astype(jnp.float32) for entry in floats))
    result, pullback = jax.vjp(forward, *floats)
    grads = pullback(cotangent.astype(jnp.float32))
    return (result.astype(jnp.bfloat16), grads[0].astype(jnp.bfloat16), grads[1], grads[2], grads[3], grads[4], grads[5], grads[6], grads[7], grads[8], grads[9], grads[10])
```

```python
import jax
import jax.numpy as jnp
from jax import lax
from jax.sharding import PartitionSpec as P

HEAD_DIM = 128
GROUPS = 3
TP = 4


highest = lax.Precision.HIGHEST
bfloat = jnp.bfloat16
single = jnp.float32


def layer_norm(values):
    centred = values - jnp.mean(values, axis=-1, keepdims=True)
    return centred * lax.rsqrt(jnp.mean(centred * centred, axis=-1, keepdims=True) + 1e-06)


def slot_tables(device, slot_count, image_device, image_offset, image_length, image_group):
    slot_ids = jnp.arange(slot_count, dtype=jnp.int32)[:, None]
    starts = image_offset[None, :]
    inside = (
        (image_device[None, :] == device)
        & (slot_ids >= starts)
        & (slot_ids < starts + image_length[None, :])
    )
    numbers = jnp.arange(image_device.shape[0], dtype=jnp.int32)[None, :]
    segment = jnp.sum(jnp.where(inside, numbers + 1, 0), axis=1) - 1
    usable = jnp.any(inside, axis=1)
    group_slot = jnp.sum(jnp.where(inside, image_group[None, :], 0), axis=1)
    onehot = (group_slot[:, None] == jnp.arange(GROUPS, dtype=jnp.int32)[None, :]) & usable[:, None]
    return (segment, usable.astype(single), onehot.astype(single))


def dot(left, right, contract):
    return lax.dot_general(left, right, (contract, ((), ())), preferred_element_type=single)


def mm(left, right):
    return dot(left, right, ((1,), (0,)))


def mm_t(left, right):
    return dot(left, right, ((1,), (1,)))


def t_mm(left, right):
    return dot(left, right, ((0,), (0,)))


def body(
    tokens,
    noise_embed,
    qkv_weight,
    out_weight,
    out_bias,
    up_weight,
    up_bias,
    down_weight,
    down_bias,
    mod_weight,
    mod_bias,
    cotangent,
    image_device,
    image_offset,
    image_length,
    image_group,
):
    n = lax.axis_size("wide")
    cores = lax.axis_size("narrow")
    wide = lax.axis_index("wide")
    core = lax.axis_index("narrow")
    rows, width = tokens.shape
    shard = qkv_weight.shape[0]
    ff = up_weight.shape[1]
    ff_shard = ff // n
    low = n // 8
    members = n // TP
    bit_y, bit_l, bit_h = n // 8, n // 4, n // 2
    tp_masks = (0, bit_y, bit_l, bit_l | bit_y)
    low_masks = []
    mask = low // 2
    while mask >= 1:
        low_masks.append(mask)
        mask //= 2
    dp_masks = [bit_h] + low_masks

    def pw(value, mask):
        return lax.ppermute(value, "wide", [(i, i ^ mask) for i in range(n)])

    def pc(value, mask):
        return lax.ppermute(value, "narrow", [(i, i ^ mask) for i in range(cores)])

    def position(index):
        return (index // bit_y) % TP

    def member(index):
        return (index // bit_h) * low + index % low

    tp_self = position(wide)
    dp_self = member(wide)

    def take(value, index, axis):
        return lax.dynamic_index_in_dim(value, index, axis, keepdims=False)

    def cut(value, index, axis, parts):
        size = value.shape[axis] // parts
        return lax.dynamic_slice_in_dim(value, index * size, size, axis)

    def member_gather(piece):
        pieces = {0: piece}
        for mask in dp_masks:
            for key in list(pieces):
                pieces[key | mask] = pw(pieces[key], mask)
        return pieces

    def core_gather(pieces):
        result = [pieces]
        for step in range(1, cores):
            result.append({key: pc(pieces[key], step) for key in pieces})
        return result

    def tp_gather(value):
        half = value.shape[0] // 2
        from_y = pw(value, bit_y)
        from_l = pw(value, bit_l)
        first = pw(from_l[:half], bit_y)
        second = pw(from_y[half:], bit_l)
        return [value, from_y, from_l, jnp.concatenate([first, second], axis=0)]

    def tp_scatter(blocks):
        own, for_y, for_l, far = blocks
        half = own.shape[0] // 2
        first = pw(far[:half].astype(bfloat), bit_y)
        second = pw(far[half:].astype(bfloat), bit_l)
        l_low = pw(for_l[half:].astype(bfloat), bit_l)
        y_low = pw(for_y[:half].astype(bfloat), bit_y)
        l_high = pw((for_l[:half].astype(single) + first.astype(single)).astype(bfloat), bit_l)
        y_high = pw((for_y[half:].astype(single) + second.astype(single)).astype(bfloat), bit_y)
        from_l = jnp.concatenate([l_high, l_low], axis=0).astype(single)
        from_y = jnp.concatenate([y_low, y_high], axis=0).astype(single)
        return own.astype(single) + from_l + from_y

    def tp_exchange(blocks):
        return [blocks[0]] + [pw(block, mask) for block, mask in zip(blocks[1:], tp_masks[1:])]

    def sum_all(value, with_cores):
        if with_cores:
            step = 1
            while step < cores:
                value = value + pc(value, step)
                step *= 2
        step = 1
        while step < n:
            value = value + pw(value, step)
            step *= 2
        return value

    def absolute(blocks):
        return jnp.stack(
            [
                lax.select_n(tp_self, *[blocks[place ^ option] for option in range(TP)])
                for place in range(TP)
            ]
        )

    silu_low = jax.nn.silu(noise_embed).astype(bfloat)
    emb_rows = mod_weight.shape[0]
    silu_rows = lax.dynamic_slice_in_dim(silu_low, wide * emb_rows, emb_rows, 1)
    mod_part = mm(silu_rows, mod_weight)
    bias_rows = mod_bias.shape[0]
    mod_columns = jnp.zeros((mod_weight.shape[1],), single)
    mod_columns = lax.dynamic_update_slice_in_dim(
        mod_columns, mod_bias.astype(single), wide * bias_rows, 0
    )
    mod_part = mod_part + mod_columns[None, :]

    def spread(value, total):
        return lax.dynamic_update_slice_in_dim(
            jnp.zeros((total,), single), value.astype(single), wide * value.shape[0], 0
        )

    first_part = mod_part[:, : 2 * width].reshape(-1, 128)
    second_part = jnp.concatenate(
        [
            mod_part[:, 2 * width :].reshape(-1),
            spread(out_bias, width),
            spread(down_bias, width),
            spread(up_bias, ff),
        ]
    ).reshape(-1, 128)
    first_sum = sum_all(first_part, False).reshape(GROUPS, 2 * width)
    second_sum = sum_all(second_part, False).reshape(-1)
    rest = second_sum[: GROUPS * 4 * width].reshape(GROUPS, 4 * width)
    biases = second_sum[GROUPS * 4 * width :]
    out_bias_full = biases[:width]
    down_bias_full = biases[width : 2 * width]
    up_bias_full = biases[2 * width :]

    feature = 2 * (width // 8)
    feature_core = feature // cores

    def qkv_chunk(place):
        view = qkv_weight.reshape(shard, 3, 2, TP, width // 8)
        picked = take(view, place, 3).reshape(shard, 3, cores, feature_core)
        return take(picked, core, 2).reshape(shard, 3 * feature_core)

    def up_chunk(place):
        view = up_weight.reshape(shard, 2, TP, low, cores, ff_shard // cores)
        picked = take(view, place, 2)
        return take(picked, core, 3).reshape(shard, members * (ff_shard // cores))

    def rows_gathered(chunk_of):
        pieces = tp_exchange([chunk_of(position(wide ^ mask)) for mask in tp_masks])
        stacked = absolute(pieces)
        gathered = core_gather(member_gather(stacked))
        result = []
        for parts in gathered:
            buffer = jnp.zeros((2, TP, low) + stacked.shape[1:], bfloat)
            for mask, piece in parts.items():
                index = wide ^ mask
                buffer = lax.dynamic_update_slice(
                    buffer, piece[None, :, None], (index // bit_h, 0, index % low, 0, 0)
                )
            result.append(buffer.reshape(width, stacked.shape[2]))
        return result

    def members_placed(parts):
        sample = parts[0]
        buffer = jnp.zeros((members,) + sample.shape, bfloat)
        for mask, piece in parts.items():
            buffer = lax.dynamic_update_slice_in_dim(buffer, piece[None], member(wide ^ mask), 0)
        return buffer.reshape((members * sample.shape[0],) + sample.shape[1:])

    out_half = cut(out_weight, core, 1, cores)
    out_stack = members_placed(member_gather(out_half))
    out_own = tp_gather(out_stack)
    out_parts = core_gather(dict(enumerate(out_own)))
    qkv_parts = rows_gathered(qkv_chunk)
    up_parts = rows_gathered(up_chunk)
    down_half = cut(down_weight, core, 0, cores)
    down_parts = [members_placed(parts) for parts in core_gather(member_gather(down_half))]

    device = wide * cores + core
    segment, usable, onehot = slot_tables(
        device, rows, image_device, image_offset, image_length, image_group
    )
    same = []
    for mask in tp_masks:
        seg = slot_tables(
            (wide ^ mask) * cores + core, rows, image_device, image_offset, image_length, image_group
        )[0]
        same.append(seg[:, None] == seg[None, :])
    same = jnp.stack(same)

    def per_row(table):
        return jnp.dot(onehot, table, precision=highest, preferred_element_type=single)

    shift_a, scale_a = jnp.split(per_row(first_sum), 2, axis=1)
    gate_a, shift_b, scale_b, gate_b = jnp.split(per_row(rest), 4, axis=1)

    x_rows = tokens.astype(single)
    normed_a = layer_norm(x_rows)
    modulated_a = (normed_a * (1.0 + scale_a) + shift_a).astype(bfloat)
    all_a = jnp.concatenate(tp_gather(modulated_a), axis=0)
    grad_out = cotangent.astype(single) * usable[:, None]
    grad_branch_b = (gate_b * grad_out).astype(bfloat)
    heads = feature_core // HEAD_DIM
    scale_factor = HEAD_DIM ** (-0.5)
    attn = []
    for weight in qkv_parts:
        projected = mm(all_a, weight).astype(bfloat)
        view = projected.reshape(TP, rows, 3, heads, HEAD_DIM)
        queries, key_rows, value_rows = view[:, :, 0], view[:, :, 1], view[:, :, 2]
        raw = (
            jnp.einsum("bqhd,bkhd->bhqk", queries, key_rows, preferred_element_type=single)
            * scale_factor
        )
        masked = jnp.where(same[:, None], raw, -1e30)
        row_max = jnp.max(masked, axis=-1, keepdims=True)
        powers = jnp.exp(masked - row_max)
        totals = jnp.sum(powers, axis=-1, keepdims=True)
        attend = powers / totals
        log_total = row_max + jnp.log(totals)
        context = jnp.einsum(
            "bhqk,bkhd->bqhd", attend.astype(bfloat), value_rows, preferred_element_type=single
        )
        context = context.astype(bfloat).reshape(TP, rows, heads * HEAD_DIM)
        attn.append((queries, key_rows, value_rows, log_total, context))

    def core_order(values, axis):
        return jnp.concatenate(
            [
                lax.select_n(core, *[values[place ^ option] for option in range(cores)])
                for place in range(cores)
            ],
            axis=axis,
        )

    context_all = core_order([entry[4] for entry in attn], 2)
    context_own = tp_exchange([context_all[t] for t in range(TP)])
    branch_cols = []
    for step in range(cores):
        total = None
        for t in range(TP):
            term = mm(context_own[t], out_parts[step][t])
            total = term if total is None else total + term
        branch_cols.append(total)
    branch_a = core_order(branch_cols, 1) + out_bias_full
    residual = x_rows + gate_a * branch_a
    normed_b = layer_norm(residual)
    modulated_b = (normed_b * (1.0 + scale_b) + shift_b).astype(bfloat)

    all_gb = jnp.concatenate(tp_gather(grad_branch_b), axis=0)
    all_b = jnp.concatenate(tp_gather(modulated_b), axis=0)
    up_bias_view = up_bias_full.reshape(2, TP, low, cores, ff_shard // cores)
    up_bias_here = take(up_bias_view, tp_self, 1)
    hiddens, grads_pre = [], []
    branch_b = None
    grad_mod_b = None
    for step in range(cores):
        bias = take(up_bias_here, core ^ step, 2).reshape(-1)
        hidden_pre = mm(all_b, up_parts[step]) + bias
        hidden, gelu_pull = jax.vjp(jax.nn.gelu, hidden_pre)
        hidden = hidden.astype(bfloat)
        grad_hidden = mm_t(all_gb, down_parts[step])
        grad_pre = gelu_pull(grad_hidden)[0].astype(bfloat)
        hiddens.append(hidden)
        grads_pre.append(grad_pre)
        term = mm_t(grad_pre, up_parts[step])
        grad_mod_b = term if grad_mod_b is None else grad_mod_b + term
        term = mm(hidden, down_parts[step])
        branch_b = term if branch_b is None else branch_b + term
    grad_mod_b = tp_scatter(
        [grad_mod_b[t * rows : (t + 1) * rows] for t in range(TP)]
    )
    branch_b = (
        tp_scatter([branch_b[t * rows : (t + 1) * rows] for t in range(TP)]) + down_bias_full
    )
    output = ((residual + gate_b * branch_b) * usable[:, None]).astype(bfloat)
    grad_gate_b = grad_out * branch_b

    def core_scatter(make):
        total = make(0)
        for step in range(1, cores):
            total = total + pc(make(step).astype(bfloat), step).astype(single)
        return total.astype(bfloat)

    def member_scatter(value):
        for axis_mask in reversed(low_masks):
            bit = (wide // axis_mask) % 2
            view = value.reshape((2, value.shape[1] // 2, 2) + value.shape[2:])
            keep = take(view, bit, 2)
            send = take(view, 1 - bit, 2)
            value = (keep.astype(single) + pw(send, axis_mask).astype(single)).astype(bfloat)
        value = value[:, 0]
        bit = wide // bit_h
        keep = take(value, bit, 0)
        send = take(value, 1 - bit, 0)
        return keep.astype(single) + pw(send, bit_h).astype(single)

    def core_spread(value):
        value = value.astype(bfloat)
        return [value] + [pc(value, step) for step in range(1, cores)]

    down_total = core_scatter(lambda step: t_mm(hiddens[step], all_gb))
    down_sum = member_scatter(down_total.reshape(2, low, ff_shard // cores, width))
    down_grad = core_order(core_spread(down_sum), 0).astype(single)

    def row_sum(value, columns_of):
        view = value.reshape(2, TP, low, shard, value.shape[1])
        mine = member_scatter(jnp.swapaxes(view, 1, 2))
        blocks = [take(mine, position(wide ^ mask), 0).astype(bfloat) for mask in tp_masks]
        received = absolute(tp_exchange(blocks))
        spread_out = core_spread(received)
        return columns_of(spread_out)

    def up_columns(parts):
        views = [
            part.reshape(TP, shard, 2, low, 1, ff_shard // cores) for part in parts
        ]
        joined = core_order(views, 4)
        return jnp.transpose(joined, (1, 2, 0, 3, 4, 5)).reshape(shard, ff).astype(single)

    def qkv_columns(parts):
        views = [part.reshape(TP, shard, 3, 1, feature_core) for part in parts]
        joined = core_order(views, 3).reshape(TP, shard, 3, 2, width // 8)
        return jnp.transpose(joined, (1, 2, 3, 0, 4)).reshape(shard, 3 * width).astype(single)

    up_total = core_scatter(lambda step: t_mm(all_b, grads_pre[step]))
    up_grad = row_sum(up_total, up_columns)
    up_bias_term = [jnp.sum(grad_pre.astype(single), axis=0) for grad_pre in grads_pre]
    down_bias_term = jnp.sum(grad_branch_b.astype(single), axis=0)

    grad_scale_b = grad_mod_b * normed_b
    norm_pull_b = jax.vjp(layer_norm, residual)[1]
    grad_resid = grad_out + norm_pull_b(grad_mod_b * (1.0 + scale_b))[0]
    grad_gate_a = grad_resid * branch_a
    grad_branch_a = (gate_a * grad_resid).astype(bfloat)
    out_bias_term = jnp.sum(grad_branch_a.astype(single), axis=0)
    branch_parts = [cut(grad_branch_a, core ^ step, 1, cores) for step in range(cores)]
    grad_context_blocks = []
    for t in range(TP):
        total = None
        for step in range(cores):
            term = mm_t(branch_parts[step], out_parts[step][t])
            total = term if total is None else total + term
        grad_context_blocks.append(total.astype(bfloat))
    grad_context_all = jnp.stack(tp_exchange(grad_context_blocks))

    context_row = jnp.concatenate(context_own, axis=1)
    out_total = core_scatter(lambda step: t_mm(context_row, branch_parts[step]))
    out_blocks = out_total.reshape(TP, members * shard, width // cores)
    out_here = tp_scatter([out_blocks[t] for t in range(TP)]).astype(bfloat)
    out_sum = member_scatter(out_here.reshape(2, low, shard, width // cores))
    out_grad = core_order(core_spread(out_sum), 1).astype(single)

    grad_projected = []
    for step, (queries, key_rows, value_rows, log_total, _) in enumerate(attn):
        grad_context = cut(grad_context_all, core ^ step, 2, cores).reshape(
            TP, rows, heads, HEAD_DIM
        )
        raw = (
            jnp.einsum("bqhd,bkhd->bhqk", queries, key_rows, preferred_element_type=single)
            * scale_factor
        )
        masked = jnp.where(same[:, None], raw, -1e30)
        attend = jnp.exp(masked - log_total)
        grad_attend = jnp.einsum(
            "bqhd,bkhd->bhqk", grad_context, value_rows, preferred_element_type=single
        )
        grad_scores = (
            attend * (grad_attend - jnp.sum(attend * grad_attend, axis=-1, keepdims=True))
        ).astype(bfloat)
        grad_queries = (
            jnp.einsum("bhqk,bkhd->bqhd", grad_scores, key_rows, preferred_element_type=single)
            * scale_factor
        )
        grad_keys = (
            jnp.einsum("bhqk,bqhd->bkhd", grad_scores, queries, preferred_element_type=single)
            * scale_factor
        )
        grad_values = jnp.einsum(
            "bhqk,bqhd->bkhd", attend.astype(bfloat), grad_context, preferred_element_type=single
        )
        stacked = jnp.stack([grad_queries, grad_keys, grad_values], axis=2).astype(bfloat)
        grad_projected.append(stacked.reshape(TP * rows, 3 * feature_core))

    grad_mod_a = None
    for step in range(cores):
        term = mm_t(grad_projected[step], qkv_parts[step])
        grad_mod_a = term if grad_mod_a is None else grad_mod_a + term
    grad_mod_a = tp_scatter([grad_mod_a[t * rows : (t + 1) * rows] for t in range(TP)])
    qkv_total = core_scatter(lambda step: t_mm(all_a, grad_projected[step]))
    qkv_grad = row_sum(qkv_total, qkv_columns)

    norm_pull_a = jax.vjp(layer_norm, x_rows)[1]
    tokens_grad = (grad_resid + norm_pull_a(grad_mod_a * (1.0 + scale_a))[0]).astype(bfloat)

    def by_group(value):
        return jnp.einsum(
            "tg,tc->gc", onehot, value, precision=highest, preferred_element_type=single
        )

    late = by_group(jnp.concatenate([grad_mod_a, grad_mod_a * normed_a], axis=1))
    early = by_group(
        jnp.concatenate([grad_gate_a, grad_mod_b, grad_scale_b, grad_gate_b], axis=1)
    )
    up_bias_parts = core_order(
        [part.reshape(2, low, 1, ff_shard // cores) for part in up_bias_term], 2
    )
    up_bias_slot = lax.dynamic_update_slice(
        jnp.zeros((2, TP, low, cores, ff_shard // cores), single),
        up_bias_parts[:, None],
        (0, tp_self, 0, 0, 0),
    )
    early_vector = jnp.concatenate(
        [early.reshape(-1), out_bias_term, down_bias_term, up_bias_slot.reshape(-1)]
    ).reshape(-1, 128)
    early_sum = sum_all(early_vector, True).reshape(-1)
    late_sum = sum_all(late.reshape(-1, 128), True).reshape(GROUPS, 2 * width)
    early_groups = early_sum[: GROUPS * 4 * width].reshape(GROUPS, 4 * width)
    bias_sums = early_sum[GROUPS * 4 * width :]
    grad_modulation = jnp.concatenate([late_sum, early_groups], axis=1).astype(bfloat)

    out_bias_grad = cut(bias_sums[:width], wide, 0, n)
    down_bias_grad = cut(bias_sums[width : 2 * width], wide, 0, n)
    up_bias_grad = cut(bias_sums[2 * width :], wide, 0, n)

    noise_rows = lax.dynamic_slice_in_dim(noise_embed, wide * emb_rows, emb_rows, 1)
    mod_grad = jnp.einsum("ge,gc->ec", silu_rows, grad_modulation, preferred_element_type=single)
    mod_bias_grad = lax.dynamic_slice_in_dim(
        jnp.sum(grad_modulation.astype(single), axis=0), wide * bias_rows, bias_rows, 0
    )
    grad_silu = jnp.einsum("gc,ec->ge", grad_modulation, mod_weight, preferred_element_type=single)
    silu_pull = jax.vjp(jax.nn.silu, noise_rows)[1]
    noise_grad = silu_pull(grad_silu)[0]
    return (
        output,
        tokens_grad,
        noise_grad,
        qkv_grad,
        out_grad,
        out_bias_grad,
        up_grad,
        up_bias_grad,
        down_grad,
        down_bias_grad,
        mod_grad,
        mod_bias_grad,
    )


def solution(mesh):
    return jax.shard_map(
        body,
        mesh=mesh,
        in_specs=(
            P(("wide", "narrow"), None),
            P(),
            P("wide", None),
            P("wide", None),
            P("wide"),
            P("wide", None),
            P("wide"),
            P("wide", None),
            P("wide"),
            P("wide", None),
            P("wide"),
            P(("wide", "narrow"), None),
            P(),
            P(),
            P(),
            P(),
        ),
        out_specs=(
            P(("wide", "narrow"), None),
            P(("wide", "narrow"), None),
            P(None, "wide"),
            P("wide", None),
            P("wide", None),
            P("wide"),
            P("wide", None),
            P("wide"),
            P("wide", None),
            P("wide"),
            P("wide", None),
            P("wide"),
        ),
        check_vma=False,
    )
```
